32 devices in a mesh: kpt: 8 (over z, core), row: 4 (over y, x).
Axes of the slice: x: 2, y: 2, z: 4, core: 2. Of those that a mesh axis runs over, the one named last changes fastest.
Arguments:
- occ_orbitals: bfloat16 [32, 2048, 128], P('kpt', 'row'), may hold values from -0.5 to 0.5
- virt_orbitals: bfloat16 [32, 2048, 256], P('kpt', 'row'), may hold values from -0.375 to 0.375
- occ_gap: bfloat16 [32, 128], P('kpt'), may hold values from 0.049804688 to 3
- virt_gap: bfloat16 [32, 256], P('kpt'), may hold values from 0.049804688 to 3
- partner: int32 [3, 32], replicated, may hold values from 0 to 31, as said below
Outputs:
- chi: float32 [3, 4, 2048, 2048], P(None, None, 'row', 'kpt')
The draws below stay inside these ranges and needn't reach their ends.
Inputs may be any that keep to these rules, and one draw needn't show every extreme that they name: For each transfer q there is a shift s_q of 0 to 4 with partner[q, k] = (k - s_q) mod 32 for every k; the shifts of different transfers differ, and some transfer has s_q = 4.
All inputs are finite; a program needn't handle non-finite values.
Results may differ from the reference program's by a relative error of at most 0.0003.
Values may be sent and summed in bfloat16 or wider, within the bound.
A program may use at most 384 MiB of HBM per device.

```python
import math
import jax
import jax.numpy as jnp
from jax import lax

NP = 2048
NOCC = 128
NV = 256
NTAU = 4
QWIN = 3
K_DEV = 4
K = 32


def draw_partner(key, part):
    others = jax.random.permutation(jax.random.fold_in(key, 7), jnp.arange(K_DEV, dtype=jnp.int32))[:QWIN - 1].astype(jnp.int32)
    shift_values = jnp.concatenate([jnp.full((1,), K_DEV, jnp.int32), others])
    shift_values = jax.random.permutation(jax.random.fold_in(key, 11), shift_values).astype(jnp.int32)
    momentum_ids = jnp.arange(K, dtype=jnp.int32)
    return ((momentum_ids[None, :] - shift_values[:, None]) % K).astype(jnp.int32)


def levels(rng, extent, pieces, least, high):
    def one(dim, blocks):
        steps = jax.random.uniform(jax.random.fold_in(jax.random.fold_in(rng, 6), dim), (blocks,), jnp.float32, least / len(pieces), high / len(pieces))
        return jnp.repeat(jnp.exp(steps), extent[dim] // blocks).reshape((-1,) + (1,) * (len(extent) - dim - 1))

    gain = one(*pieces[0])
    for cut in pieces[1:]:
        gain = gain * one(*cut)
    return gain


def normal_values(own_key, extent, deviation, most, pieces=(), kind=jnp.bfloat16):
    drawn = jax.random.normal(own_key, extent, jnp.float32) * deviation
    if len(pieces) > 0:
        drawn = levels(own_key, extent, pieces, -0.22, 0.18) * drawn
    return jnp.clip(drawn, min=-most, max=most).astype(kind)


def setup_inputs(seed: int = 0) -> dict:
    seeds = jax.random.split(jax.random.key(seed), 6)
    occ_orbitals = normal_values(seeds[0], (K, NP, NOCC), NOCC ** -0.5, 0.5, ((0, 8), (1, 4)))
    virt_orbitals = normal_values(seeds[1], (K, NP, NV), NV ** -0.5, 0.375, ((0, 8), (1, 4)))
    occ_gap = jnp.clip(jnp.exp(math.log(3.0) - 4.0982585 * jax.random.uniform(seeds[2], (K, NOCC), jnp.float32) ** levels(seeds[2], (K, NOCC), ((0, 8),), -0.2, 0.2)), 0.049804688, 3.0).astype(jnp.bfloat16)
    virt_gap = jnp.clip(jnp.exp(math.log(3.0) - 4.0982585 * jax.random.uniform(seeds[3], (K, NV), jnp.float32) ** levels(seeds[3], (K, NV), ((0, 8),), -0.2, 0.2)), 0.049804688, 3.0).astype(jnp.bfloat16)
    partner = draw_partner(jax.random.fold_in(seeds[5], 71), 0)
    return dict(occ_orbitals=occ_orbitals, virt_orbitals=virt_orbitals, occ_gap=occ_gap, virt_gap=virt_gap, partner=partner)


def reference(occ_orbitals, virt_orbitals, occ_gap, virt_gap, partner):
    tau_values = 0.25 * 2.0 ** jnp.arange(NTAU, dtype=jnp.float32)
    momentum_ids = jnp.arange(K, dtype=jnp.int32)
    results = []
    for step_index in range(NTAU):
        moment = tau_values[step_index]

        def accumulate(running, momentum):
            occ_rows = occ_orbitals[momentum]
            occ_factor = jnp.exp(-occ_gap[momentum].astype(jnp.float32) * moment)
            occ_panel = (occ_rows.astype(jnp.float32) * occ_factor[None, :]).astype(jnp.bfloat16)
            occ_green = jnp.dot(occ_panel, occ_rows.T, preferred_element_type=jnp.float32)
            updated = []
            for transfer in range(QWIN):
                partner_id = partner[transfer, momentum]
                virt_rows = virt_orbitals[partner_id]
                virt_factor = jnp.exp(-virt_gap[partner_id].astype(jnp.float32) * moment)
                virt_panel = (virt_rows.astype(jnp.float32) * virt_factor[None, :]).astype(jnp.bfloat16)
                virt_green = jnp.dot(virt_panel, virt_rows.T, preferred_element_type=jnp.float32)
                updated.append(running[transfer] + occ_green * virt_green)
            return jnp.stack(updated), None

        running, _ = lax.scan(accumulate, jnp.zeros((QWIN, NP, NP), jnp.float32), momentum_ids)
        results.append(running)
    return jnp.stack(results, axis=1)
```

```python
import functools

import jax
import jax.numpy as jnp
from jax import lax
from jax.experimental import pallas as pl
from jax.experimental.pallas import tpu as pltpu
from jax.sharding import PartitionSpec as P

NTAU = 4
PAD = 16
SUB = 32


def kernel(nk, nr, per, occ_ref, virt_ref, gap_ref, partner_ref, out_ref, rows, cols, og, vg,
           local_sem, row_recv, col_recv, right_send, left_send, sib_send, col_send):
    K = nk * per
    npts, nocc = occ_ref.shape[1], occ_ref.shape[2]
    nall = rows.shape[2]
    ncol = cols.shape[1]
    tile = og.shape[1]
    j = lax.axis_index("kpt")
    i = lax.axis_index("row")
    c, s = j // 2, j % 2
    nc = nk // 2
    cpr = nk // nr
    root = j // cpr
    off = pl.multiple_of((j % cpr) * ncol, ncol)
    transfers = partner_ref.shape[0]

    def place(index):
        return jnp.where(index % 2 == 0, index // 2, nr - 1 - index // 2)

    def at_place(p):
        return jnp.where(p < nr // 2, 2 * p, 2 * (nr - 1 - p) + 1)

    me, top = place(i), place(root)
    ahead, behind = at_place((me + 1) % nr), at_place((me + nr - 1) % nr)
    dist_a, dist_b = (me - top + nr) % nr, (top - me + nr) % nr
    is_root = i == root
    has_right, has_left = c + 1 < nc, c > 0

    locals_ = []
    for a in range(per):
        m = j * per + a
        locals_.append((
            pltpu.make_async_copy(occ_ref.at[a], rows.at[m, pl.ds(0, npts), pl.ds(0, nocc)], local_sem.at[a, 0]),
            pltpu.make_async_copy(virt_ref.at[a], rows.at[m, pl.ds(0, npts), pl.ds(nocc, nall - nocc)], local_sem.at[a, 1]),
            pltpu.make_async_copy(gap_ref.at[a], rows.at[m, pl.ds(npts, PAD)], local_sem.at[a, 2]),
        ))
    for group in locals_:
        for copy in group:
            copy.start()

    barrier = pltpu.get_barrier_semaphore()

    def greet(device):
        pl.semaphore_signal(barrier, inc=1, device_id=device, device_id_type=pl.DeviceIdType.MESH)

    greet((j + 1 - 2 * s, i))
    greet((j, ahead))
    greet((j, behind))

    @pl.when(has_right)
    def _():
        greet((j + 2, i))

    @pl.when(has_left)
    def _():
        greet((j - 2, i))

    pl.semaphore_wait(barrier, 3 + has_right.astype(jnp.int32) + has_left.astype(jnp.int32))

    for group in locals_:
        for copy in group:
            copy.wait()

    def remote(src, dst, send, recv, device):
        return pltpu.make_async_remote_copy(src_ref=src, dst_ref=dst, send_sem=send, recv_sem=recv,
                                            device_id=device, device_id_type=pl.DeviceIdType.MESH)

    def to_right(m):
        return remote(rows.at[m], rows.at[m], right_send.at[m], row_recv.at[m], (j + 2, i))

    def to_left(m):
        return remote(rows.at[m], rows.at[m], left_send.at[m], row_recv.at[m], (j - 2, i))

    def to_sib(m):
        return remote(rows.at[m], rows.at[m], sib_send.at[m], row_recv.at[m], (j + 1 - 2 * s, i))

    def col_copy(m, device, from_root):
        src = rows.at[m, pl.ds(off, ncol)] if from_root else cols.at[m]
        return remote(src, cols.at[m], col_send.at[m], col_recv.at[m], (j, device))

    def root_copy(m):
        return pltpu.make_async_copy(rows.at[m, pl.ds(off, ncol)], cols.at[m], col_recv.at[m])

    def wait_row(m):
        pltpu.make_async_copy(rows.at[m], rows.at[m], row_recv.at[m]).wait()

    def wait_col(m):
        pltpu.make_async_copy(cols.at[m], cols.at[m], col_recv.at[m]).wait()

    def root_send(m, start):
        @pl.when(is_root)
        def _():
            if start:
                root_copy(m).start()
            for parity, device in ((0, ahead), (1, behind)):
                @pl.when(m % 2 == parity)
                def _():
                    copy = col_copy(m, device, True)
                    copy.start() if start else copy.wait_send()

    def row_stage(f, start):
        h, a = f // per, f % per

        def go(copy):
            copy.start() if start else copy.wait_send()

        @pl.when(h == 0)
        def _():
            m = j * per + a

            @pl.when(has_right)
            def _():
                go(to_right(m))

            @pl.when(has_left)
            def _():
                go(to_left(m))

            go(to_sib(m))
            root_send(m, start)

        for left in (True, False):
            there = (c - h >= 0) if left else (c + h < nc)
            src = (c - h) if left else (c + h)
            onward = has_right if left else has_left

            @pl.when(there & (h > 0))
            def _():
                m = (2 * src + s) * per + a
                if start:
                    wait_row(m)

                @pl.when(onward)
                def _():
                    go(to_right(m) if left else to_left(m))

                go(to_sib(m))
                root_send(m, start)

        for left in (True, False):
            there = (c - h >= 0) if left else ((c + h < nc) & (h > 0))
            src = (c - h) if left else (c + h)

            @pl.when(there)
            def _():
                m = (2 * src + 1 - s) * per + a
                if start:
                    wait_row(m)
                root_send(m, start)

    def col_stage(f, start):
        h, a = f // per, f % per
        for left in (True, False):
            there = (c - h >= 0) if left else ((c + h < nc) & (h > 0))
            src = (c - h) if left else (c + h)
            for core in range(2):
                @pl.when(there & jnp.logical_not(is_root))
                def _():
                    m = (2 * src + core) * per + a
                    if start:
                        wait_col(m)
                    for parity, dist, device in ((0, dist_a, ahead), (1, dist_b, behind)):
                        @pl.when((m % 2 == parity) & (dist < nr - 1))
                        def _():
                            copy = col_copy(m, device, False)
                            copy.start() if start else copy.wait_send()

    total = nc * per

    def step(f, carry):
        @pl.when(f < total)
        def _():
            row_stage(f, True)

        @pl.when(f > 0)
        def _():
            col_stage(f - 1, True)

        return carry

    lax.fori_loop(0, total + 1, step, 0)

    def root_done(m, carry):
        @pl.when(is_root)
        def _():
            wait_col(m)

        return carry

    lax.fori_loop(0, K, root_done, 0)

    tiles = npts // tile
    contract = (((1,), (1,)), ((), ()))

    def block(g, carry):
        t, r0 = g % NTAU, pl.multiple_of((g // NTAU) * tile, tile)
        moment = jnp.where(t == 0, 0.25, jnp.where(t == 1, 0.5, jnp.where(t == 2, 1.0, 2.0))).astype(jnp.float32)

        def one(k, inner):
            gap = rows[k, pl.ds(npts, PAD), :].astype(jnp.float32)
            factor = jnp.exp(-gap * moment)[0:1]
            panel = (rows[k, pl.ds(r0, tile), :].astype(jnp.float32) * factor).astype(jnp.bfloat16)
            column = cols[k]
            og[k] = lax.dot_general(panel[:, :nocc], column[:, :nocc], contract, preferred_element_type=jnp.float32)
            vg[k] = lax.dot_general(panel[:, nocc:], column[:, nocc:], contract, preferred_element_type=jnp.float32)
            return inner

        lax.fori_loop(0, K, one, 0, unroll=2)

        def piece(p, inner):
            here = pl.ds(pl.multiple_of(p * SUB, SUB), SUB)

            def add(k, sums):
                occ = og[k, here, :]
                return tuple(x + occ * vg[partner_ref[q, k], here, :] for q, x in enumerate(sums))

            zero = jnp.zeros((SUB, ncol), jnp.float32)
            sums = lax.fori_loop(0, K, add, (zero,) * transfers, unroll=4)
            for q in range(transfers):
                out_ref[q, t, pl.ds(pl.multiple_of(r0 + p * SUB, SUB), SUB), :] = sums[q]
            return inner

        lax.fori_loop(0, tile // SUB, piece, 0)
        return carry

    lax.fori_loop(0, tiles * NTAU, block, 0)

    def finish(f, carry):
        row_stage(f, False)
        col_stage(f, False)
        return carry

    lax.fori_loop(0, total, finish, 0)


def on_device(nk, nr, occ_orbitals, virt_orbitals, occ_gap, virt_gap, partner):
    per, npts, nocc = occ_orbitals.shape
    nv = virt_orbitals.shape[2]
    K, ncol, nall = nk * per, npts * nr // nk, nocc + nv
    tile = min(256, npts)
    transfers = partner.shape[0]
    gaps = jnp.broadcast_to(jnp.concatenate([occ_gap, virt_gap], axis=1)[:, None, :], (per, PAD, nall))
    dma = pltpu.SemaphoreType.DMA
    return pl.pallas_call(
        functools.partial(kernel, nk, nr, per),
        out_shape=jax.ShapeDtypeStruct((transfers, NTAU, npts, ncol), jnp.float32),
        in_specs=[pl.BlockSpec(memory_space=pl.ANY)] * 3 + [pl.BlockSpec(memory_space=pltpu.SMEM)],
        out_specs=pl.BlockSpec(memory_space=pltpu.VMEM),
        scratch_shapes=[
            pltpu.VMEM((K, npts + PAD, nall), jnp.bfloat16),
            pltpu.VMEM((K, ncol, nall), jnp.bfloat16),
            pltpu.VMEM((K, tile, ncol), jnp.float32),
            pltpu.VMEM((K, tile, ncol), jnp.float32),
            dma((per, 3)), dma((K,)), dma((K,)), dma((K,)), dma((K,)), dma((K,)), dma((K,)),
        ],
        compiler_params=pltpu.CompilerParams(
            collective_id=0, has_side_effects=True, vmem_limit_bytes=60 * 2**20),
    )(occ_orbitals, virt_orbitals, gaps, partner)


def solution(mesh):
    in_specs = (P("kpt", "row", None), P("kpt", "row", None), P("kpt", None), P("kpt", None), P())
    out_specs = P(None, None, "row", "kpt")
    return jax.shard_map(
        functools.partial(on_device, mesh.shape["kpt"], mesh.shape["row"]),
        mesh=mesh, in_specs=in_specs, out_specs=out_specs, check_vma=False,
    )
```

```python
import functools

import jax
import jax.numpy as jnp
from jax import lax
from jax.experimental import pallas as pl
from jax.experimental.pallas import tpu as pltpu
from jax.sharding import PartitionSpec as P

NTAU = 4
PAD = 16
SUB = 32
LAG = 1


def kernel(nk, nr, per, occ_ref, virt_ref, gap_ref, partner_ref, out_ref, rows, cols, og, vg,
           local_sem, row_recv, col_recv, right_send, left_send, sib_send, col_send):
    K = nk * per
    npts, nocc = occ_ref.shape[1], occ_ref.shape[2]
    nall = rows.shape[2]
    ncol = cols.shape[1]
    tile = og.shape[1]
    j = lax.axis_index("kpt")
    i = lax.axis_index("row")
    c, s = j // 2, j % 2
    nc = nk // 2
    cpr = nk // nr
    root = j // cpr
    off = pl.multiple_of((j % cpr) * ncol, ncol)
    transfers = partner_ref.shape[0]

    def place(index):
        return jnp.where(index % 2 == 0, index // 2, nr - 1 - index // 2)

    def at_place(p):
        return jnp.where(p < nr // 2, 2 * p, 2 * (nr - 1 - p) + 1)

    me, top = place(i), place(root)
    ahead, behind = at_place((me + 1) % nr), at_place((me + nr - 1) % nr)
    dist_a, dist_b = (me - top + nr) % nr, (top - me + nr) % nr
    is_root = i == root
    has_right, has_left = c + 1 < nc, c > 0

    locals_ = []
    for a in range(per):
        m = j * per + a
        locals_.append((
            pltpu.make_async_copy(occ_ref.at[a], rows.at[m, pl.ds(0, npts), pl.ds(0, nocc)], local_sem.at[a, 0]),
            pltpu.make_async_copy(virt_ref.at[a], rows.at[m, pl.ds(0, npts), pl.ds(nocc, nall - nocc)], local_sem.at[a, 1]),
            pltpu.make_async_copy(gap_ref.at[a], rows.at[m, pl.ds(npts, PAD)], local_sem.at[a, 2]),
        ))
    for group in locals_:
        for copy in group:
            copy.start()

    barrier = pltpu.get_barrier_semaphore()

    def greet(device):
        pl.semaphore_signal(barrier, inc=1, device_id=device, device_id_type=pl.DeviceIdType.MESH)

    greet((j + 1 - 2 * s, i))
    greet((j, ahead))
    greet((j, behind))

    @pl.when(has_right)
    def _():
        greet((j + 2, i))

    @pl.when(has_left)
    def _():
        greet((j - 2, i))

    pl.semaphore_wait(barrier, 3 + has_right.astype(jnp.int32) + has_left.astype(jnp.int32))

    for group in locals_:
        for copy in group:
            copy.wait()

    def remote(src, dst, send, recv, device):
        return pltpu.make_async_remote_copy(src_ref=src, dst_ref=dst, send_sem=send, recv_sem=recv,
                                            device_id=device, device_id_type=pl.DeviceIdType.MESH)

    def to_right(m):
        return remote(rows.at[m], rows.at[m], right_send.at[m], row_recv.at[m], (j + 2, i))

    def to_left(m):
        return remote(rows.at[m], rows.at[m], left_send.at[m], row_recv.at[m], (j - 2, i))

    def to_sib(m):
        return remote(rows.at[m], rows.at[m], sib_send.at[m], row_recv.at[m], (j + 1 - 2 * s, i))

    def col_copy(m, device, from_root):
        src = rows.at[m, pl.ds(off, ncol)] if from_root else cols.at[m]
        return remote(src, cols.at[m], col_send.at[m], col_recv.at[m], (j, device))

    def root_copy(m):
        return pltpu.make_async_copy(rows.at[m, pl.ds(off, ncol)], cols.at[m], col_recv.at[m])

    def wait_row(m):
        pltpu.make_async_copy(rows.at[m], rows.at[m], row_recv.at[m]).wait()

    def wait_col(m):
        pltpu.make_async_copy(cols.at[m], cols.at[m], col_recv.at[m]).wait()

    def way(m):
        return (m + m // per) % 2

    def root_send(m, start):
        @pl.when(is_root)
        def _():
            if start:
                root_copy(m).start()
            for parity, device in ((0, ahead), (1, behind)):
                @pl.when(way(m) == parity)
                def _():
                    copy = col_copy(m, device, True)
                    copy.start() if start else copy.wait_send()

    def row_stage(f, start):
        h, a = f // per, f % per

        def go(copy):
            copy.start() if start else copy.wait_send()

        @pl.when(h == 0)
        def _():
            m = j * per + a

            @pl.when(has_right)
            def _():
                go(to_right(m))

            @pl.when(has_left)
            def _():
                go(to_left(m))

            go(to_sib(m))
            root_send(m, start)

        for left in (True, False):
            there = (c - h >= 0) if left else (c + h < nc)
            src = (c - h) if left else (c + h)
            onward = has_right if left else has_left

            @pl.when(there & (h > 0))
            def _():
                m = (2 * src + s) * per + a
                if start:
                    wait_row(m)

                @pl.when(onward)
                def _():
                    go(to_right(m) if left else to_left(m))

                go(to_sib(m))
                root_send(m, start)

        for left in (True, False):
            there = (c - h >= 0) if left else ((c + h < nc) & (h > 0))
            src = (c - h) if left else (c + h)

            @pl.when(there)
            def _():
                m = (2 * src + 1 - s) * per + a
                if start:
                    wait_row(m)
                root_send(m, start)

    def col_stage(f, start, parity, dist, device):
        h, a = f // per, f % per
        for left in (True, False):
            there = (c - h >= 0) if left else ((c + h < nc) & (h > 0))
            src = (c - h) if left else (c + h)
            for core in range(2):
                m = (2 * src + core) * per + a

                @pl.when(there & (way(m) == parity) & (dist > 0) & (dist < nr - 1))
                def _():
                    if start:
                        wait_col(m)
                    copy = col_copy(m, device, False)
                    copy.start() if start else copy.wait_send()

    total = nc * per
    ways = ((0, dist_a, ahead), (1, dist_b, behind))

    def step(f, carry):
        @pl.when(f < total)
        def _():
            row_stage(f, True)

        for parity, dist, device in ways:
            then = f - LAG * dist

            @pl.when((then >= 0) & (then < total))
            def _():
                col_stage(then, True, parity, dist, device)

        return carry

    lax.fori_loop(0, total + LAG * (nr - 2), step, 0)

    def col_done(m, carry):
        for parity, dist, _ in ways:
            @pl.when((way(m) == parity) & ((dist == 0) | (dist == nr - 1)))
            def _():
                wait_col(m)

        return carry

    lax.fori_loop(0, K, col_done, 0)

    tiles = npts // tile
    contract = (((1,), (1,)), ((), ()))

    def block(g, carry):
        t, r0 = g % NTAU, pl.multiple_of((g // NTAU) * tile, tile)
        moment = jnp.where(t == 0, 0.25, jnp.where(t == 1, 0.5, jnp.where(t == 2, 1.0, 2.0))).astype(jnp.float32)

        def one(k, inner):
            gap = rows[k, pl.ds(npts, PAD), :].astype(jnp.float32)
            factor = jnp.exp(-gap * moment)[0:1]
            panel = (rows[k, pl.ds(r0, tile), :].astype(jnp.float32) * factor).astype(jnp.bfloat16)
            column = cols[k]
            og[k] = lax.dot_general(panel[:, :nocc], column[:, :nocc], contract, preferred_element_type=jnp.float32)
            vg[k] = lax.dot_general(panel[:, nocc:], column[:, nocc:], contract, preferred_element_type=jnp.float32)
            return inner

        lax.fori_loop(0, K, one, 0, unroll=2)

        def piece(p, inner):
            here = pl.ds(pl.multiple_of(p * SUB, SUB), SUB)

            def add(k, sums):
                occ = og[k, here, :]
                return tuple(x + occ * vg[partner_ref[q, k], here, :] for q, x in enumerate(sums))

            zero = jnp.zeros((SUB, ncol), jnp.float32)
            sums = lax.fori_loop(0, K, add, (zero,) * transfers, unroll=4)
            for q in range(transfers):
                out_ref[q, t, pl.ds(pl.multiple_of(r0 + p * SUB, SUB), SUB), :] = sums[q]
            return inner

        lax.fori_loop(0, tile // SUB, piece, 0)
        return carry

    lax.fori_loop(0, tiles * NTAU, block, 0)

    def finish(f, carry):
        row_stage(f, False)
        for parity, dist, device in ways:
            col_stage(f, False, parity, dist, device)
        return carry

    lax.fori_loop(0, total, finish, 0)


def on_device(nk, nr, occ_orbitals, virt_orbitals, occ_gap, virt_gap, partner):
    per, npts, nocc = occ_orbitals.shape
    nv = virt_orbitals.shape[2]
    K, ncol, nall = nk * per, npts * nr // nk, nocc + nv
    tile = min(256, npts)
    transfers = partner.shape[0]
    gaps = jnp.broadcast_to(jnp.concatenate([occ_gap, virt_gap], axis=1)[:, None, :], (per, PAD, nall))
    dma = pltpu.SemaphoreType.DMA
    return pl.pallas_call(
        functools.partial(kernel, nk, nr, per),
        out_shape=jax.ShapeDtypeStruct((transfers, NTAU, npts, ncol), jnp.float32),
        in_specs=[pl.BlockSpec(memory_space=pl.ANY)] * 3 + [pl.BlockSpec(memory_space=pltpu.SMEM)],
        out_specs=pl.BlockSpec(memory_space=pltpu.VMEM),
        scratch_shapes=[
            pltpu.VMEM((K, npts + PAD, nall), jnp.bfloat16),
            pltpu.VMEM((K, ncol, nall), jnp.bfloat16),
            pltpu.VMEM((K, tile, ncol), jnp.float32),
            pltpu.VMEM((K, tile, ncol), jnp.float32),
            dma((per, 3)), dma((K,)), dma((K,)), dma((K,)), dma((K,)), dma((K,)), dma((K,)),
        ],
        compiler_params=pltpu.CompilerParams(
            collective_id=0, has_side_effects=True, vmem_limit_bytes=60 * 2**20),
    )(occ_orbitals, virt_orbitals, gaps, partner)


def solution(mesh):
    in_specs = (P("kpt", "row", None), P("kpt", "row", None), P("kpt", None), P("kpt", None), P())
    out_specs = P(None, None, "row", "kpt")
    return jax.shard_map(
        functools.partial(on_device, mesh.shape["kpt"], mesh.shape["row"]),
        mesh=mesh, in_specs=in_specs, out_specs=out_specs, check_vma=False,
    )
```

```python
import functools

import jax
import jax.numpy as jnp
from jax import lax
from jax.experimental import pallas as pl
from jax.experimental.pallas import tpu as pltpu
from jax.sharding import PartitionSpec as P

NTAU = 4
PAD = 16
SUB = 32
LAG = 1


def kernel(nk, nr, per, occ_ref, virt_ref, gap_ref, partner_ref, out_ref, rows, cols, og, vg,
           local_sem, row_recv, col_recv, right_send, left_send, sib_send, col_send):
    K = nk * per
    npts, nocc = occ_ref.shape[1], occ_ref.shape[2]
    nall = rows.shape[2]
    ncol = cols.shape[1]
    j = lax.axis_index("kpt")
    i = lax.axis_index("row")
    c, s = j // 2, j % 2
    nc = nk // 2
    cpr = nk // nr
    root = j // cpr
    off = pl.multiple_of((j % cpr) * ncol, ncol)
    transfers = partner_ref.shape[0]

    def place(index):
        return jnp.where(index % 2 == 0, index // 2, nr - 1 - index // 2)

    def at_place(p):
        return jnp.where(p < nr // 2, 2 * p, 2 * (nr - 1 - p) + 1)

    me, top = place(i), place(root)
    ahead, behind = at_place((me + 1) % nr), at_place((me + nr - 1) % nr)
    dist_a, dist_b = (me - top + nr) % nr, (top - me + nr) % nr
    is_root = i == root
    has_right, has_left = c + 1 < nc, c > 0

    locals_ = []
    for a in range(per):
        m = j * per + a
        locals_.append((
            pltpu.make_async_copy(occ_ref.at[a], rows.at[m, pl.ds(0, npts), pl.ds(0, nocc)], local_sem.at[a, 0]),
            pltpu.make_async_copy(virt_ref.at[a], rows.at[m, pl.ds(0, npts), pl.ds(nocc, nall - nocc)], local_sem.at[a, 1]),
            pltpu.make_async_copy(gap_ref.at[a], rows.at[m, pl.ds(npts, PAD)], local_sem.at[a, 2]),
        ))
    for group in locals_:
        for copy in group:
            copy.start()

    barrier = pltpu.get_barrier_semaphore()

    def greet(device):
        pl.semaphore_signal(barrier, inc=1, device_id=device, device_id_type=pl.DeviceIdType.MESH)

    greet((j + 1 - 2 * s, i))
    greet((j, ahead))
    greet((j, behind))

    @pl.when(has_right)
    def _():
        greet((j + 2, i))

    @pl.when(has_left)
    def _():
        greet((j - 2, i))

    pl.semaphore_wait(barrier, 3 + has_right.astype(jnp.int32) + has_left.astype(jnp.int32))

    for group in locals_:
        for copy in group:
            copy.wait()

    def remote(src, dst, send, recv, device):
        return pltpu.make_async_remote_copy(src_ref=src, dst_ref=dst, send_sem=send, recv_sem=recv,
                                            device_id=device, device_id_type=pl.DeviceIdType.MESH)

    def to_right(m):
        return remote(rows.at[m], rows.at[m], right_send.at[m], row_recv.at[m], (j + 2, i))

    def to_left(m):
        return remote(rows.at[m], rows.at[m], left_send.at[m], row_recv.at[m], (j - 2, i))

    def to_sib(m):
        return remote(rows.at[m], rows.at[m], sib_send.at[m], row_recv.at[m], (j + 1 - 2 * s, i))

    def col_copy(m, device, from_root):
        src = rows.at[m, pl.ds(off, ncol)] if from_root else cols.at[m]
        return remote(src, cols.at[m], col_send.at[m], col_recv.at[m], (j, device))

    def root_copy(m):
        return pltpu.make_async_copy(rows.at[m, pl.ds(off, ncol)], cols.at[m], col_recv.at[m])

    def wait_row(m):
        pltpu.make_async_copy(rows.at[m], rows.at[m], row_recv.at[m]).wait()

    def wait_col(m):
        pltpu.make_async_copy(cols.at[m], cols.at[m], col_recv.at[m]).wait()

    def way(m):
        return (m + m // per) % 2

    def root_send(m, start):
        @pl.when(is_root)
        def _():
            if start:
                root_copy(m).start()
            for parity, device in ((0, ahead), (1, behind)):
                @pl.when(way(m) == parity)
                def _():
                    copy = col_copy(m, device, True)
                    copy.start() if start else copy.wait_send()

    def row_stage(f, start):
        h, a = f // per, f % per

        def go(copy):
            copy.start() if start else copy.wait_send()

        @pl.when(h == 0)
        def _():
            m = j * per + a

            @pl.when(has_right)
            def _():
                go(to_right(m))

            @pl.when(has_left)
            def _():
                go(to_left(m))

            go(to_sib(m))
            root_send(m, start)

        for left in (True, False):
            there = (c - h >= 0) if left else (c + h < nc)
            src = (c - h) if left else (c + h)
            onward = has_right if left else has_left

            @pl.when(there & (h > 0))
            def _():
                m = (2 * src + s) * per + a
                if start:
                    wait_row(m)

                @pl.when(onward)
                def _():
                    go(to_right(m) if left else to_left(m))

                go(to_sib(m))
                root_send(m, start)

        for left in (True, False):
            there = (c - h >= 0) if left else ((c + h < nc) & (h > 0))
            src = (c - h) if left else (c + h)

            @pl.when(there)
            def _():
                m = (2 * src + 1 - s) * per + a
                if start:
                    wait_row(m)
                root_send(m, start)

    contract = (((1,), (1,)), ((), ()))

    def green(k, moment):
        gap = rows[k, pl.ds(npts, PAD), :].astype(jnp.float32)[0:1]
        factor = jnp.exp(-gap * moment)
        panel = (rows[k, pl.ds(0, npts), :].astype(jnp.float32) * factor).astype(jnp.bfloat16)
        column = cols[k]
        og[k] = lax.dot_general(panel[:, :nocc], column[:, :nocc], contract, preferred_element_type=jnp.float32)
        vg[k] = lax.dot_general(panel[:, nocc:], column[:, nocc:], contract, preferred_element_type=jnp.float32)

    def green_stage(f):
        h, a = f // per, f % per
        for left in (True, False):
            there = (c - h >= 0) if left else ((c + h < nc) & (h > 0))
            src = (c - h) if left else (c + h)

            @pl.when(there)
            def _():
                for core in range(2):
                    green((2 * src + core) * per + a, 0.25)

    def col_stage(f, start, parity, dist, device):
        h, a = f // per, f % per
        for left in (True, False):
            there = (c - h >= 0) if left else ((c + h < nc) & (h > 0))
            src = (c - h) if left else (c + h)
            for core in range(2):
                m = (2 * src + core) * per + a

                @pl.when(there & (way(m) == parity))
                def _():
                    if start:
                        wait_col(m)

                    @pl.when((dist > 0) & (dist < nr - 1))
                    def _():
                        copy = col_copy(m, device, False)
                        copy.start() if start else copy.wait_send()

    total = nc * per
    ways = ((0, dist_a, ahead), (1, dist_b, behind))

    def step(f, carry):
        @pl.when(f < total)
        def _():
            row_stage(f, True)

        for parity, dist, device in ways:
            then = f - LAG * jnp.maximum(dist, 1)

            @pl.when((then >= 0) & (then < total))
            def _():
                col_stage(then, True, parity, dist, device)

        ready = f - LAG * (nr - 1)

        @pl.when(ready >= 0)
        def _():
            green_stage(ready)

        return carry

    lax.fori_loop(0, total + LAG * (nr - 1), step, 0)

    def block(t, carry):
        @pl.when(t > 0)
        def _():
            moment = jnp.where(t == 1, 0.5, jnp.where(t == 2, 1.0, 2.0)).astype(jnp.float32)

            def one(k, inner):
                green(k, moment)
                return inner

            lax.fori_loop(0, K, one, 0, unroll=8)

        def piece(p, inner):
            here = pl.ds(pl.multiple_of(p * SUB, SUB), SUB)

            def add(k, sums):
                occ = og[k, here, :]
                return tuple(x + occ * vg[partner_ref[q, k], here, :] for q, x in enumerate(sums))

            zero = jnp.zeros((SUB, ncol), jnp.float32)
            sums = lax.fori_loop(0, K, add, (zero,) * transfers, unroll=16)
            for q in range(transfers):
                out_ref[q, t, here, :] = sums[q]
            return inner

        lax.fori_loop(0, npts // SUB, piece, 0)
        return carry

    lax.fori_loop(0, NTAU, block, 0)

    def finish(f, carry):
        row_stage(f, False)
        for parity, dist, device in ways:
            col_stage(f, False, parity, dist, device)
        return carry

    lax.fori_loop(0, total, finish, 0)


def on_device(nk, nr, occ_orbitals, virt_orbitals, occ_gap, virt_gap, partner):
    per, npts, nocc = occ_orbitals.shape
    nv = virt_orbitals.shape[2]
    K, ncol, nall = nk * per, npts * nr // nk, nocc + nv
    tile = npts
    transfers = partner.shape[0]
    gaps = jnp.broadcast_to(jnp.concatenate([occ_gap, virt_gap], axis=1)[:, None, :], (per, PAD, nall))
    dma = pltpu.SemaphoreType.DMA
    return pl.pallas_call(
        functools.partial(kernel, nk, nr, per),
        out_shape=jax.ShapeDtypeStruct((transfers, NTAU, npts, ncol), jnp.float32),
        in_specs=[pl.BlockSpec(memory_space=pl.ANY)] * 3 + [pl.BlockSpec(memory_space=pltpu.SMEM)],
        out_specs=pl.BlockSpec(memory_space=pltpu.VMEM),
        scratch_shapes=[
            pltpu.VMEM((K, npts + PAD, nall), jnp.bfloat16),
            pltpu.VMEM((K, ncol, nall), jnp.bfloat16),
            pltpu.VMEM((K, tile, ncol), jnp.float32),
            pltpu.VMEM((K, tile, ncol), jnp.float32),
            dma((per, 3)), dma((K,)), dma((K,)), dma((K,)), dma((K,)), dma((K,)), dma((K,)),
        ],
        compiler_params=pltpu.CompilerParams(
            collective_id=0, has_side_effects=True, vmem_limit_bytes=62 * 2**20),
    )(occ_orbitals, virt_orbitals, gaps, partner)


def solution(mesh):
    in_specs = (P("kpt", "row", None), P("kpt", "row", None), P("kpt", None), P("kpt", None), P())
    out_specs = P(None, None, "row", "kpt")
    return jax.shard_map(
        functools.partial(on_device, mesh.shape["kpt"], mesh.shape["row"]),
        mesh=mesh, in_specs=in_specs, out_specs=out_specs, check_vma=False,
    )
```

```python
import functools

import jax
import jax.numpy as jnp
from jax import lax
from jax.experimental import pallas as pl
from jax.experimental.pallas import tpu as pltpu
from jax.sharding import PartitionSpec as P

NTAU = 4
PAD = 16
SUB = 32
LAG = 1


def kernel(nk, nr, per, occ_ref, virt_ref, gap_ref, partner_ref, out_ref, rows, cols, og, vg, stage, out_sem,
           local_sem, row_recv, col_recv, right_send, left_send, sib_send, col_send):
    K = nk * per
    npts, nocc = occ_ref.shape[1], occ_ref.shape[2]
    nall = rows.shape[2]
    ncol = cols.shape[1]
    j = lax.axis_index("kpt")
    i = lax.axis_index("row")
    c, s = j // 2, j % 2
    nc = nk // 2
    cpr = nk // nr
    root = j // cpr
    off = pl.multiple_of((j % cpr) * ncol, ncol)
    transfers = partner_ref.shape[0]

    def place(index):
        return jnp.where(index % 2 == 0, index // 2, nr - 1 - index // 2)

    def at_place(p):
        return jnp.where(p < nr // 2, 2 * p, 2 * (nr - 1 - p) + 1)

    me, top = place(i), place(root)
    ahead, behind = at_place((me + 1) % nr), at_place((me + nr - 1) % nr)
    dist_a, dist_b = (me - top + nr) % nr, (top - me + nr) % nr
    is_root = i == root
    has_right, has_left = c + 1 < nc, c > 0

    locals_ = []
    for a in range(per):
        m = j * per + a
        locals_.append((
            pltpu.make_async_copy(occ_ref.at[a], rows.at[m, pl.ds(0, npts), pl.ds(0, nocc)], local_sem.at[a, 0]),
            pltpu.make_async_copy(virt_ref.at[a], rows.at[m, pl.ds(0, npts), pl.ds(nocc, nall - nocc)], local_sem.at[a, 1]),
            pltpu.make_async_copy(gap_ref.at[a], rows.at[m, pl.ds(npts, PAD)], local_sem.at[a, 2]),
        ))
    for group in locals_:
        for copy in group:
            copy.start()

    barrier = pltpu.get_barrier_semaphore()

    def greet(device):
        pl.semaphore_signal(barrier, inc=1, device_id=device, device_id_type=pl.DeviceIdType.MESH)

    greet((j + 1 - 2 * s, i))
    greet((j, ahead))
    greet((j, behind))

    @pl.when(has_right)
    def _():
        greet((j + 2, i))

    @pl.when(has_left)
    def _():
        greet((j - 2, i))

    pl.semaphore_wait(barrier, 3 + has_right.astype(jnp.int32) + has_left.astype(jnp.int32))

    for group in locals_:
        for copy in group:
            copy.wait()

    def remote(src, dst, send, recv, device):
        return pltpu.make_async_remote_copy(src_ref=src, dst_ref=dst, send_sem=send, recv_sem=recv,
                                            device_id=device, device_id_type=pl.DeviceIdType.MESH)

    def to_right(m):
        return remote(rows.at[m], rows.at[m], right_send.at[m], row_recv.at[m], (j + 2, i))

    def to_left(m):
        return remote(rows.at[m], rows.at[m], left_send.at[m], row_recv.at[m], (j - 2, i))

    def to_sib(m):
        return remote(rows.at[m], rows.at[m], sib_send.at[m], row_recv.at[m], (j + 1 - 2 * s, i))

    def col_copy(m, device, from_root):
        src = rows.at[m, pl.ds(off, ncol)] if from_root else cols.at[m]
        return remote(src, cols.at[m], col_send.at[m], col_recv.at[m], (j, device))

    def root_copy(m):
        return pltpu.make_async_copy(rows.at[m, pl.ds(off, ncol)], cols.at[m], col_recv.at[m])

    def wait_row(m):
        pltpu.make_async_copy(rows.at[m], rows.at[m], row_recv.at[m]).wait()

    def wait_col(m):
        pltpu.make_async_copy(cols.at[m], cols.at[m], col_recv.at[m]).wait()

    def way(m):
        return (m + m // per) % 2

    def root_send(m, start):
        @pl.when(is_root)
        def _():
            if start:
                root_copy(m).start()
            for parity, device in ((0, ahead), (1, behind)):
                @pl.when(way(m) == parity)
                def _():
                    copy = col_copy(m, device, True)
                    copy.start() if start else copy.wait_send()

    def row_stage(f, start):
        h, a = f // per, f % per

        def go(copy):
            copy.start() if start else copy.wait_send()

        @pl.when(h == 0)
        def _():
            m = j * per + a

            @pl.when(has_right)
            def _():
                go(to_right(m))

            @pl.when(has_left)
            def _():
                go(to_left(m))

            go(to_sib(m))
            root_send(m, start)

        for left in (True, False):
            there = (c - h >= 0) if left else (c + h < nc)
            src = (c - h) if left else (c + h)
            onward = has_right if left else has_left

            @pl.when(there & (h > 0))
            def _():
                m = (2 * src + s) * per + a
                if start:
                    wait_row(m)

                @pl.when(onward)
                def _():
                    go(to_right(m) if left else to_left(m))

                go(to_sib(m))
                root_send(m, start)

        for left in (True, False):
            there = (c - h >= 0) if left else ((c + h < nc) & (h > 0))
            src = (c - h) if left else (c + h)

            @pl.when(there)
            def _():
                m = (2 * src + 1 - s) * per + a
                if start:
                    wait_row(m)
                root_send(m, start)

    contract = (((1,), (1,)), ((), ()))

    def green(k, moment):
        gap = rows[k, pl.ds(npts, PAD), :].astype(jnp.float32)[0:1]
        factor = jnp.exp(-gap * moment)
        panel = (rows[k, pl.ds(0, npts), :].astype(jnp.float32) * factor).astype(jnp.bfloat16)
        column = cols[k]
        og[k] = lax.dot_general(panel[:, :nocc], column[:, :nocc], contract, preferred_element_type=jnp.float32)
        vg[k] = lax.dot_general(panel[:, nocc:], column[:, nocc:], contract, preferred_element_type=jnp.float32)

    def green_stage(f):
        h, a = f // per, f % per
        for left in (True, False):
            there = (c - h >= 0) if left else ((c + h < nc) & (h > 0))
            src = (c - h) if left else (c + h)

            @pl.when(there)
            def _():
                for core in range(2):
                    green((2 * src + core) * per + a, 0.25)

    def col_stage(f, start, parity, dist, device):
        h, a = f // per, f % per
        for left in (True, False):
            there = (c - h >= 0) if left else ((c + h < nc) & (h > 0))
            src = (c - h) if left else (c + h)
            for core in range(2):
                m = (2 * src + core) * per + a

                @pl.when(there & (way(m) == parity))
                def _():
                    if start:
                        wait_col(m)

                    @pl.when((dist > 0) & (dist < nr - 1))
                    def _():
                        copy = col_copy(m, device, False)
                        copy.start() if start else copy.wait_send()

    total = nc * per
    ways = ((0, dist_a, ahead), (1, dist_b, behind))

    def step(f, carry):
        @pl.when(f < total)
        def _():
            row_stage(f, True)

        for parity, dist, device in ways:
            then = f - LAG * jnp.maximum(dist, 1)

            @pl.when((then >= 0) & (then < total))
            def _():
                col_stage(then, True, parity, dist, device)

        ready = f - LAG * (nr - 1)

        @pl.when(ready >= 0)
        def _():
            green_stage(ready)

        return carry

    lax.fori_loop(0, total + LAG * (nr - 1), step, 0)

    def out_copy(t):
        return pltpu.make_async_copy(stage.at[t % 2], out_ref.at[:, t], out_sem.at[t % 2])

    def block(t, carry):
        @pl.when(t > 1)
        def _():
            out_copy(t - 2).wait()

        @pl.when(t > 0)
        def _():
            moment = jnp.where(t == 1, 0.5, jnp.where(t == 2, 1.0, 2.0)).astype(jnp.float32)

            def one(k, inner):
                green(k, moment)
                return inner

            lax.fori_loop(0, K, one, 0, unroll=8)

        def piece(p, inner):
            here = pl.ds(pl.multiple_of(p * SUB, SUB), SUB)

            def add(k, sums):
                occ = og[k, here, :]
                return tuple(x + occ * vg[partner_ref[q, k], here, :] for q, x in enumerate(sums))

            zero = jnp.zeros((SUB, ncol), jnp.float32)
            sums = lax.fori_loop(0, K, add, (zero,) * transfers, unroll=16)
            for q in range(transfers):
                stage[t % 2, q, here, :] = sums[q]
            return inner

        lax.fori_loop(0, npts // SUB, piece, 0)
        out_copy(t).start()
        return carry

    lax.fori_loop(0, NTAU, block, 0)
    for t in (NTAU - 2, NTAU - 1):
        out_copy(t).wait()

    def finish(f, carry):
        row_stage(f, False)
        for parity, dist, device in ways:
            col_stage(f, False, parity, dist, device)
        return carry

    lax.fori_loop(0, total, finish, 0)


def on_device(nk, nr, occ_orbitals, virt_orbitals, occ_gap, virt_gap, partner):
    per, npts, nocc = occ_orbitals.shape
    nv = virt_orbitals.shape[2]
    K, ncol, nall = nk * per, npts * nr // nk, nocc + nv
    tile = npts
    transfers = partner.shape[0]
    gaps = jnp.broadcast_to(jnp.concatenate([occ_gap, virt_gap], axis=1)[:, None, :], (per, PAD, nall))
    dma = pltpu.SemaphoreType.DMA
    return pl.pallas_call(
        functools.partial(kernel, nk, nr, per),
        out_shape=jax.ShapeDtypeStruct((transfers, NTAU, npts, ncol), jnp.float32),
        in_specs=[pl.BlockSpec(memory_space=pl.ANY)] * 3 + [pl.BlockSpec(memory_space=pltpu.SMEM)],
        out_specs=pl.BlockSpec(memory_space=pl.ANY),
        scratch_shapes=[
            pltpu.VMEM((K, npts + PAD, nall), jnp.bfloat16),
            pltpu.VMEM((K, ncol, nall), jnp.bfloat16),
            pltpu.VMEM((K, tile, ncol), jnp.float32),
            pltpu.VMEM((K, tile, ncol), jnp.float32),
            pltpu.VMEM((2, transfers, npts, ncol), jnp.float32), dma((2,)),
            dma((per, 3)), dma((K,)), dma((K,)), dma((K,)), dma((K,)), dma((K,)), dma((K,)),
        ],
        compiler_params=pltpu.CompilerParams(
            collective_id=0, has_side_effects=True, vmem_limit_bytes=62 * 2**20),
    )(occ_orbitals, virt_orbitals, gaps, partner)


def solution(mesh):
    in_specs = (P("kpt", "row", None), P("kpt", "row", None), P("kpt", None), P("kpt", None), P())
    out_specs = P(None, None, "row", "kpt")
    return jax.shard_map(
        functools.partial(on_device, mesh.shape["kpt"], mesh.shape["row"]),
        mesh=mesh, in_specs=in_specs, out_specs=out_specs, check_vma=False,
    )
```
